32 devices in a mesh: gx: 4 (over y, x), gy: 8 (over z, core).
Axes of the slice: x: 2, y: 2, z: 4, core: 2. Of those that a mesh axis runs over, the one named last changes fastest.
Arguments:
- tokens: bfloat16 [32, 2048, 768], P(('gx', 'gy')), may hold values from -6 to 6
- cotangent: bfloat16 [32, 2048, 768], P(('gx', 'gy')), may hold values from -6 to 6
- chosen: int32 [32, 256], P(('gx', 'gy')), may hold values from 0 to 2047, as said below
- segment: int32 [32, 2048], P(('gx', 'gy')), may hold values from 0 to 5, never falling along the last dimension, each value on 1 to 1024 neighbouring positions
- router: bfloat16 [768], P(('gx', 'gy')), may hold values from -0.21875 to 0.21875
- gain_one: bfloat16 [768], P(('gx', 'gy')), may hold values from 0.25 to 1.75
- gain_two: bfloat16 [768], P(('gx', 'gy')), may hold values from 0.25 to 1.75
- query_weight: bfloat16 [768, 768], P(('gx', 'gy')), may hold values from -0.21875 to 0.21875
- key_weight: bfloat16 [768, 768], P(('gx', 'gy')), may hold values from -0.21875 to 0.21875
- value_weight: bfloat16 [768, 768], P(('gx', 'gy')), may hold values from -0.21875 to 0.21875
- output_weight: bfloat16 [768, 768], P(('gx', 'gy')), may hold values from -0.875 to 0.875
- expand_weight: bfloat16 [768, 3072], P(('gx', 'gy')), may hold values from -0.21875 to 0.21875
- shrink_weight: bfloat16 [3072, 768], P(('gx', 'gy')), may hold values from -0.109375 to 0.109375
Outputs:
- out_tokens: bfloat16 [32, 2048, 768], P(('gx', 'gy'))
- grad_tokens: bfloat16 [32, 2048, 768], P(('gx', 'gy'))
- grad_router: float32 [768], P(('gx', 'gy'))
- grad_gain_one: float32 [768], P(('gx', 'gy'))
- grad_gain_two: float32 [768], P(('gx', 'gy'))
- grad_query: float32 [768, 768], P(('gx', 'gy'))
- grad_key: float32 [768, 768], P(('gx', 'gy'))
- grad_value: float32 [768, 768], P(('gx', 'gy'))
- grad_output: float32 [768, 768], P(('gx', 'gy'))
- grad_expand: float32 [768, 3072], P(('gx', 'gy'))
- grad_shrink: float32 [3072, 768], P(('gx', 'gy'))
The draws below stay inside these ranges and needn't reach their ends.
Inputs may be any that keep to these rules, and one draw needn't show every extreme that they name: `chosen`: each row holds 256 different positions of its packed row in increasing order. segment numbers never fall along a row; a segment has at most 1024 positions, one exactly that many.
All inputs are finite; a program needn't handle non-finite values.
Results may differ from the reference program's by a relative error of at most 0.011.
Values may be sent and summed in bfloat16 or wider, within the bound.
No kernel may reach another device: no remote copies, remote signals or barrier semaphores. Data moves between devices by JAX's collectives and lax.ppermute only.
A program may use at most 192 MiB of HBM per device.

```python
import math
import jax
import jax.numpy as jnp
import numpy as np
from jax import lax

D = 768
HEADS = 12
HEAD_DIM = 64
FF = 3072
SEQ = 2048
KEEP = 256
ROWS = 32


def draw_chosen(key, part):
    row_keys = jax.random.split(key, ROWS)

    def one_row(row_key):
        shuffled = jax.random.permutation(row_key, SEQ)
        return jnp.sort(shuffled[:KEEP])
    return jax.vmap(one_row)(row_keys).astype(jnp.int32)


def strengthened(values, rng, source, target, parts, factor):
    def block_of(dim):
        return (jnp.arange(values.shape[dim]) // (values.shape[dim] // parts)).reshape((-1,) + (1,) * (values.ndim - 1 - dim))

    near = jax.random.permutation(rng, parts)[block_of(target)]
    far = (block_of(target) + parts // 2) % parts
    return jnp.where((block_of(source) == near) | (block_of(source) == far), factor * values, values)


def block_scale(own_key, dims, pieces, smallest, high):
    def one(dim, parts):
        heights = jax.random.uniform(jax.random.fold_in(jax.random.fold_in(own_key, 6), dim), (parts,), jnp.float32, smallest / len(pieces), high / len(pieces))
        return jnp.repeat(jnp.exp(heights), dims[dim] // parts).reshape((-1,) + (1,) * (len(dims) - dim - 1))

    factor_of = one(*pieces[0])
    for cut in pieces[1:]:
        factor_of = factor_of * one(*cut)
    return factor_of


def profile(count, total, reach, skew):
    weights = [(1 << 20) // math.isqrt(grade ** skew) + 1 for grade in range(2, count + 1)]
    rest, holding = total - reach - (count - 1), [1] * (count - 1)
    while rest > 0:
        candidates = [i for i in range(count - 1) if holding[i] < reach]
        mass, remaining = sum([weights[i] for i in candidates]), rest
        for i in candidates:
            addition = min(reach - holding[i], max(1, remaining * weights[i] // mass), rest)
            holding[i] = holding[i] + addition
            rest = rest - addition
    return np.array([reach] + holding)


def uneven(stream_key, count, total, limit, skew):
    if count == 2:
        one = jax.random.randint(stream_key, (), max(1, total - limit), min(limit, total - 1) + 1)
        return jnp.stack([one, total - one])
    tallies = jnp.asarray(profile(count, total, limit, skew), jnp.int32)
    couples = (count - 1) // 2
    donor, receiver = tallies[1:1 + 2 * couples:2], tallies[2:2 + 2 * couples:2]
    room = jnp.minimum(donor - 1, limit - receiver)
    moved = jax.random.randint(jax.random.fold_in(stream_key, 1), (couples,), 0, 1 << 20) % (room + 1)
    tallies = tallies.at[1:1 + 2 * couples:2].set(donor - moved).at[2:2 + 2 * couples:2].set(receiver + moved)
    return tallies[jax.random.permutation(jax.random.fold_in(stream_key, 2), count)]


def normal_values(own_key, extent, deviation, limit, shards=(), held_as=jnp.bfloat16):
    entries = jax.random.normal(own_key, extent, jnp.float32) * deviation
    if len(shards) > 0:
        entries = block_scale(own_key, extent, shards, -0.22, 0.18) * entries
    return jnp.clip(entries, min=-limit, max=limit).astype(held_as)


def noise_with(key, shape, scale, bound, cuts, heavy, held_as=jnp.bfloat16):
    array = scale * jax.random.normal(key, shape, jnp.float32)
    if cuts:
        array = array * block_scale(key, shape, cuts, -0.22, 0.18)
    return jnp.clip(strengthened(array, jax.random.fold_in(key, 3), *heavy), -bound, bound).astype(held_as)


def setup_inputs(seed: int = 0) -> dict:
    key_of = jax.random.split(jax.random.key(seed), 14)
    return {
        "tokens": noise_with(key_of[0], (ROWS, SEQ, D), 1.0, 6.0, ((0, 32),), (0, 2, 32, 2.75)),
        "cotangent": noise_with(key_of[1], (ROWS, SEQ, D), 1.0, 6.0, ((0, 32),), (0, 2, 32, 2.75)),
        "chosen": draw_chosen(jax.random.fold_in(key_of[13], 71), 0),
        "segment": jax.vmap(lambda own: jnp.searchsorted(jnp.cumsum(uneven(own, 6, SEQ, SEQ // 2, 1)), jnp.arange(SEQ), side="right"))(jax.random.split(key_of[3], ROWS)).reshape((ROWS, SEQ)).astype(jnp.int32),
        "router": normal_values(key_of[4], (D,), D ** -0.5, 0.21875, ((0, 32),)),
        "gain_one": jnp.clip(1.0 + 0.15 * jax.random.normal(key_of[5], (D,), jnp.float32), 0.25, 1.75).astype(jnp.bfloat16),
        "gain_two": jnp.clip(1.0 + 0.15 * jax.random.normal(key_of[6], (D,), jnp.float32), 0.25, 1.75).astype(jnp.bfloat16),
        "query_weight": normal_values(key_of[7], (D, D), D ** -0.5, 0.21875, ((0, 32),)),
        "key_weight": normal_values(key_of[8], (D, D), D ** -0.5, 0.21875, ((0, 32),)),
        "value_weight": normal_values(key_of[9], (D, D), D ** -0.5, 0.21875, ((0, 32),)),
        "output_weight": normal_values(key_of[10], (D, D), (D // 16) ** -0.5, 0.875, ((0, 32),)),
        "expand_weight": normal_values(key_of[11], (D, FF), D ** -0.5, 0.21875, ((0, 32),)),
        "shrink_weight": normal_values(key_of[12], (FF, D), FF ** -0.5, 0.109375, ((0, 32),)),
    }


HIGHEST = lax.Precision.HIGHEST
SCALE = 0.125
EPS = 1e-06
NEGATIVE = -1e+30

@jax.custom_vjp
def low(v):
    return lax.optimization_barrier(v.astype(jnp.bfloat16)).astype(jnp.float32)

@jax.custom_vjp
def low_back(v):
    return v

def low_keep(v):
    return (low(v), None)

def low_pass(kept, grad):
    return (grad,)

def back_keep(v):
    return (v, None)

def back_low(kept, grad):
    return (low(grad),)
low.defvjp(low_keep, low_pass)
low_back.defvjp(back_keep, back_low)

def matmul(left, right):
    return jnp.dot(left, right, precision=HIGHEST)

def rms_norm(values, gain):
    return values * lax.rsqrt(lax.optimization_barrier(jnp.mean(values * values, axis=-1, keepdims=True)) + EPS) * gain

def layer_row(weights, whole, picked, seg_row):
    router, gain_one, gain_two, query_weight, key_weight, value_weight, output_weight, expand_weight, shrink_weight = weights
    hidden = whole[picked]
    router_gate = jax.nn.sigmoid(low_back(matmul(hidden, router)))
    normed = low(rms_norm(hidden, gain_one))
    queries = low(low_back(matmul(normed, query_weight))).reshape(KEEP, HEADS, HEAD_DIM)
    key_rows = low(low_back(matmul(normed, key_weight))).reshape(KEEP, HEADS, HEAD_DIM)
    value_rows = low(low_back(matmul(normed, value_weight))).reshape(KEEP, HEADS, HEAD_DIM)
    scores = low_back(jnp.einsum('qhd,khd->hqk', queries, key_rows, precision=HIGHEST) * SCALE)
    labels = seg_row[picked]
    allowed = (picked[None, :] <= picked[:, None]) & (labels[None, :] == labels[:, None])
    attn_probs = low(jax.nn.softmax(jnp.where(allowed[None], scores, NEGATIVE), axis=-1))
    attn_mixed = low(low_back(jnp.einsum('hqk,khd->qhd', attn_probs, value_rows, precision=HIGHEST))).reshape(KEEP, D)
    attn_out = low_back(matmul(attn_mixed, output_weight))
    middle = hidden + attn_out
    normed_two = low(rms_norm(middle, gain_two))
    activated = low(jax.nn.gelu(low_back(matmul(normed_two, expand_weight)), approximate=True))
    mlp_out = low_back(matmul(activated, shrink_weight))
    updated = hidden + router_gate[:, None] * (attn_out + mlp_out)
    return whole.at[picked].set(updated)

def reference(tokens, cotangent, chosen, segment, router, gain_one, gain_two, query_weight, key_weight, value_weight, output_weight, expand_weight, shrink_weight):
    params = tuple((weight.astype(jnp.float32) for weight in (router, gain_one, gain_two, query_weight, key_weight, value_weight, output_weight, expand_weight, shrink_weight)))

    def one_row(totals, inputs):
        token_row, cot_row, picked, seg_row = inputs

        def forward(weights, whole):
            return layer_row(weights, whole, picked, seg_row)
        result, pullback = jax.vjp(forward, params, token_row.astype(jnp.float32))
        weight_grads, grad_row = pullback(cot_row.astype(jnp.float32))
        totals = jax.tree.map(jnp.add, totals, weight_grads)
        return (totals, (result.astype(jnp.bfloat16), grad_row.astype(jnp.bfloat16)))
    empty_grads = jax.tree.map(jnp.zeros_like, params)
    totals, outputs = lax.scan(one_row, empty_grads, (tokens, cotangent, chosen, segment))
    return (outputs[0], outputs[1], totals[0], totals[1], totals[2], totals[3], totals[4], totals[5], totals[6], totals[7], totals[8])
```

```python
from functools import partial

import jax
import jax.numpy as jnp
from jax import lax
from jax.sharding import PartitionSpec as P

HEAD_DIM = 64


SCALE = 0.125
EPS = 1e-06
NEGATIVE = -1e30


def rms_norm(values, gain):
    return values * lax.rsqrt(jnp.mean(values * values, axis=-1, keepdims=True) + EPS) * gain


def matmul(left, right):
    return jnp.dot(left, right, preferred_element_type=jnp.float32)


def matmul_left_t(left, right):
    return lax.dot_general(
        left, right, (((0,), (0,)), ((), ())), preferred_element_type=jnp.float32
    )


def matmul_right_t(left, right):
    return lax.dot_general(
        left, right, (((1,), (1,)), ((), ())), preferred_element_type=jnp.float32
    )


GX, GY = "gx", "gy"


def mesh_bits(sizes):
    return [
        (axis, bit)
        for axis in (GX, GY)
        for bit in reversed(range(sizes[axis].bit_length() - 1))
    ]


def orders(sizes):
    low = [(GX, 0)] if sizes[GX] > 1 else []
    high = [(GX, bit) for bit in reversed(range(1, sizes[GX].bit_length() - 1))]
    line = [(GY, bit) for bit in reversed(range(1, sizes[GY].bit_length() - 1))]
    core = [(GY, 0)] if sizes[GY] > 1 else []
    return (
        low + line + high + core,
        high + line + low + core,
        line + low + high + core,
        line + high + low + core,
    )


def swap(value, sizes, stage):
    axis, bit = stage
    pairs = [(i, i ^ (1 << bit)) for i in range(sizes[axis])]
    return lax.ppermute(value, axis, pairs)


def own_bit(stage):
    axis, bit = stage
    return (lax.axis_index(axis) >> bit) & 1


def gather(shard, sizes, order):
    natural = mesh_bits(sizes)
    current = shard.reshape((1,) * len(natural) + shard.shape)
    for stage in order:
        dim = natural.index(stage)
        other = swap(current, sizes, stage)
        upper = own_bit(stage) == 1
        current = jnp.where(
            upper,
            jnp.concatenate([other, current], dim),
            jnp.concatenate([current, other], dim),
        )
    return current.reshape((-1,) + shard.shape[1:])


def scatter_sum(full, sizes, order):
    natural = mesh_bits(sizes)
    count = 1 << len(natural)
    current = full.reshape((2,) * len(natural) + (full.shape[0] // count,) + full.shape[1:])
    for stage in reversed(order):
        dim = natural.index(stage)
        mine = own_bit(stage)
        sent = lax.dynamic_index_in_dim(current, 1 - mine, dim).astype(jnp.bfloat16)
        kept = lax.dynamic_index_in_dim(current, mine, dim)
        current = kept + swap(sent, sizes, stage).astype(jnp.float32)
    return current.reshape((full.shape[0] // count,) + full.shape[1:])


def split3(array):
    width = array.shape[1]
    third = width // 3
    return [array[:, i * third : (i + 1) * third] for i in range(3)]


def body(
    sizes,
    tokens,
    cotangent,
    chosen,
    segment,
    router,
    gain_one,
    gain_two,
    query_weight,
    key_weight,
    value_weight,
    output_weight,
    expand_weight,
    shrink_weight,
):
    order = orders(sizes)
    small = jnp.stack([router, gain_one, gain_two], axis=1)
    small = jnp.pad(small, ((0, 0), (0, 128 - small.shape[1])))
    first = [
        jnp.concatenate([query_weight, small], axis=1),
        key_weight,
        value_weight,
    ]
    query_small, key_all, value_all = [gather(first[i], sizes, order[i]) for i in range(3)]
    query_all = query_small[:, : query_weight.shape[1]]
    small_all = query_small[:, query_weight.shape[1] :]
    router_all, gain_one_all, gain_two_all = [small_all[:, i] for i in range(3)]
    second = [
        jnp.concatenate([o, e], axis=1)
        for o, e in zip(split3(output_weight), split3(expand_weight))
    ]
    out_part = output_weight.shape[1] // 3
    alternate = (order[0], order[1], order[3])
    second_all = [gather(second[i], sizes, alternate[i]) for i in range(3)]
    output_parts = [part[:, :out_part] for part in second_all]
    expand_parts = [part[:, out_part:] for part in second_all]
    shrink_parts = [gather(part, sizes, order[i]) for i, part in enumerate(split3(shrink_weight))]
    output_all = jnp.concatenate(output_parts, axis=1)
    expand_all = jnp.concatenate(expand_parts, axis=1)
    shrink_all = jnp.concatenate(shrink_parts, axis=1)
    row_count, seq_len, width = tokens.shape
    keep_count = chosen.shape[1]
    head_size = HEAD_DIM
    head_count = width // head_size
    token_count = row_count * keep_count
    row_ids = jnp.arange(row_count, dtype=jnp.int32)[:, None]
    hidden_low = tokens[row_ids, chosen].reshape(token_count, width)
    hidden = hidden_low.astype(jnp.float32)
    router_gate = jax.nn.sigmoid(matmul(hidden_low, router_all))
    normed = rms_norm(hidden, gain_one_all.astype(jnp.float32)).astype(jnp.bfloat16)
    head_shape = (row_count, keep_count, head_count, head_size)
    queries = matmul(normed, query_all).astype(jnp.bfloat16).reshape(head_shape)
    key_rows = matmul(normed, key_all).astype(jnp.bfloat16).reshape(head_shape)
    value_rows = matmul(normed, value_all).astype(jnp.bfloat16).reshape(head_shape)
    labels = jnp.take_along_axis(segment, chosen, axis=1)
    allowed = (
        (chosen[:, None, :] <= chosen[:, :, None]) & (labels[:, None, :] == labels[:, :, None])
    )[:, None]

    def attn_scores():
        raw_scores = (
            jnp.einsum("rqhd,rkhd->rhqk", queries, key_rows, preferred_element_type=jnp.float32)
            * SCALE
        )
        return jnp.where(allowed, raw_scores, NEGATIVE)

    scores = attn_scores()
    peak = jnp.max(scores, axis=-1, keepdims=True)
    exp_terms = jnp.exp(scores - peak)
    total_mass = jnp.sum(exp_terms, axis=-1, keepdims=True)
    probs_low = (exp_terms / total_mass).astype(jnp.bfloat16)
    log_mass = peak + jnp.log(total_mass)
    attn_mixed = (
        jnp.einsum("rhqk,rkhd->rqhd", probs_low, value_rows, preferred_element_type=jnp.float32)
        .astype(jnp.bfloat16)
        .reshape(token_count, width)
    )
    attn_out = matmul(attn_mixed, output_all)
    middle = hidden + attn_out
    normed_two = rms_norm(middle, gain_two_all.astype(jnp.float32)).astype(jnp.bfloat16)
    pre_act = matmul(normed_two, expand_all)
    gelu_values, gelu_back = jax.vjp(partial(jax.nn.gelu, approximate=True), pre_act)
    activated = gelu_values.astype(jnp.bfloat16)
    mlp_out = matmul(activated, shrink_all)
    branch = attn_out + mlp_out
    updated = hidden + router_gate[:, None] * branch
    out_tokens = tokens.at[row_ids, chosen].set(
        updated.astype(jnp.bfloat16).reshape(row_count, keep_count, width)
    )
    router_back, gain_one_back, gain_two_back = router_all, gain_one_all, gain_two_all
    query_back, key_back, value_back, output_back = query_all, key_all, value_all, output_all
    expand_back, shrink_back = expand_all, shrink_all
    cot_rows = cotangent[row_ids, chosen].reshape(token_count, width).astype(jnp.float32)
    grad_branch = router_gate[:, None] * cot_rows
    logit_low = (jnp.sum(cot_rows * branch, axis=-1) * router_gate * (1.0 - router_gate)).astype(
        jnp.bfloat16
    )
    grad_router = matmul(logit_low, hidden_low)
    mlp_low = grad_branch.astype(jnp.bfloat16)
    grad_shrink = matmul_left_t(activated, mlp_low)
    (grad_pre,) = gelu_back(matmul_right_t(mlp_low, shrink_back))
    pre_low = grad_pre.astype(jnp.bfloat16)
    grad_expand = matmul_left_t(normed_two, pre_low)
    grad_normed_two = matmul_right_t(pre_low, expand_back)
    norm_two_value, norm_two_back = jax.vjp(rms_norm, middle, gain_two_back.astype(jnp.float32))
    grad_middle, grad_gain_two = norm_two_back(grad_normed_two)
    attn_low = (grad_middle + grad_branch).astype(jnp.bfloat16)
    grad_output = matmul_left_t(attn_mixed, attn_low)
    mixed_low = matmul_right_t(attn_low, output_back).astype(jnp.bfloat16).reshape(head_shape)
    probs_again = jnp.exp(attn_scores() - log_mass)
    probs_again_low = probs_again.astype(jnp.bfloat16)
    dvalue_low = (
        jnp.einsum(
            "rhqk,rqhd->rkhd", probs_again_low, mixed_low, preferred_element_type=jnp.float32
        )
        .astype(jnp.bfloat16)
        .reshape(token_count, width)
    )
    grad_probs = jnp.einsum(
        "rqhd,rkhd->rhqk", mixed_low, value_rows, preferred_element_type=jnp.float32
    )
    scores_low = (
        probs_again * (grad_probs - jnp.sum(probs_again * grad_probs, axis=-1, keepdims=True))
    ).astype(jnp.bfloat16)
    dquery_low = (
        (
            jnp.einsum("rhqk,rkhd->rqhd", scores_low, key_rows, preferred_element_type=jnp.float32)
            * SCALE
        )
        .astype(jnp.bfloat16)
        .reshape(token_count, width)
    )
    dkey_low = (
        (
            jnp.einsum("rhqk,rqhd->rkhd", scores_low, queries, preferred_element_type=jnp.float32)
            * SCALE
        )
        .astype(jnp.bfloat16)
        .reshape(token_count, width)
    )
    grad_query = matmul_left_t(normed, dquery_low)
    grad_key = matmul_left_t(normed, dkey_low)
    grad_value = matmul_left_t(normed, dvalue_low)
    grad_normed = (
        matmul_right_t(dquery_low, query_back)
        + matmul_right_t(dkey_low, key_back)
        + matmul_right_t(dvalue_low, value_back)
    )
    norm_one_value, norm_one_back = jax.vjp(rms_norm, hidden, gain_one_back.astype(jnp.float32))
    norm_back, grad_gain_one = norm_one_back(grad_normed)
    grad_hidden = (
        cot_rows
        + grad_middle
        + norm_back
        + logit_low.astype(jnp.float32)[:, None] * router_back.astype(jnp.float32)[None, :]
    )
    grad_tokens = cotangent.at[row_ids, chosen].set(
        grad_hidden.astype(jnp.bfloat16).reshape(row_count, keep_count, width)
    )
    shrink_share = jnp.concatenate(
        [scatter_sum(part, sizes, order[i]) for i, part in enumerate(split3(grad_shrink))], axis=1
    )
    expand_share = jnp.concatenate(
        [scatter_sum(part, sizes, alternate[i]) for i, part in enumerate(split3(grad_expand))],
        axis=1,
    )
    grad_small = jnp.stack([grad_router, grad_gain_one, grad_gain_two], axis=1)
    grad_small = jnp.pad(grad_small, ((0, 0), (0, 128 - grad_small.shape[1])))
    last = [
        jnp.concatenate([o, g], axis=1)
        for o, g in zip(
            split3(grad_output),
            (jnp.concatenate([grad_query, grad_small], axis=1), grad_key, grad_value),
        )
    ]
    last_share = [scatter_sum(part, sizes, order[i]) for i, part in enumerate(last)]
    output_share = jnp.concatenate([part[:, :out_part] for part in last_share], axis=1)
    query_share, key_share, value_share = [
        part[:, out_part : out_part + width] for part in last_share
    ]
    small_share = last_share[0][:, out_part + width :]
    shares = (
        small_share[:, 0],
        small_share[:, 1],
        small_share[:, 2],
        query_share,
        key_share,
        value_share,
        output_share,
        expand_share,
        shrink_share,
    )
    return (
        out_tokens,
        grad_tokens,
        shares[0],
        shares[1],
        shares[2],
        shares[3],
        shares[4],
        shares[5],
        shares[6],
        shares[7],
        shares[8],
    )


def solution(mesh):
    in_specs = (
        P(("gx", "gy"), None, None),
        P(("gx", "gy"), None, None),
        P(("gx", "gy"), None),
        P(("gx", "gy"), None),
        P(("gx", "gy")),
        P(("gx", "gy")),
        P(("gx", "gy")),
        P(("gx", "gy"), None),
        P(("gx", "gy"), None),
        P(("gx", "gy"), None),
        P(("gx", "gy"), None),
        P(("gx", "gy"), None),
        P(("gx", "gy"), None),
    )
    out_specs = (
        P(("gx", "gy"), None, None),
        P(("gx", "gy"), None, None),
        P(("gx", "gy")),
        P(("gx", "gy")),
        P(("gx", "gy")),
        P(("gx", "gy"), None),
        P(("gx", "gy"), None),
        P(("gx", "gy"), None),
        P(("gx", "gy"), None),
        P(("gx", "gy"), None),
        P(("gx", "gy"), None),
    )
    return jax.shard_map(partial(body, dict(mesh.shape)), mesh=mesh, in_specs=in_specs, out_specs=out_specs, check_vma=False)
```

```python
from functools import partial

import jax
import jax.numpy as jnp
from jax import lax
from jax.experimental import pallas as pl
from jax.experimental.pallas import tpu as pltpu
from jax.sharding import PartitionSpec as P

HEAD_DIM = 64


SCALE = 0.125
EPS = 1e-06
NEGATIVE = -1e30


def rms_norm(values, gain):
    return values * lax.rsqrt(jnp.mean(values * values, axis=-1, keepdims=True) + EPS) * gain


def matmul(left, right):
    return jnp.dot(left, right, preferred_element_type=jnp.float32)


def matmul_left_t(left, right):
    return lax.dot_general(
        left, right, (((0,), (0,)), ((), ())), preferred_element_type=jnp.float32
    )


def matmul_right_t(left, right):
    return lax.dot_general(
        left, right, (((1,), (1,)), ((), ())), preferred_element_type=jnp.float32
    )


GX, GY = "gx", "gy"
BOTH = (GX, GY)
LANES = 128
ATTN_ORDER = ("21yx", "12xy")
EXPAND_ORDER = ("1x2y", "2y1x")
SHRINK_ORDER = ("yx21", "y21x")


def log2(size):
    return size.bit_length() - 1


def stage_masks(sizes, order):
    low = log2(sizes[GY])
    letters = {
        "x": [low] if sizes[GX] > 1 else [],
        "y": [low + bit for bit in reversed(range(1, log2(sizes[GX])))],
        "1": [1] if low > 1 else [],
        "2": list(reversed(range(2, low))),
    }
    return tuple(tuple(bit for letter in way for bit in letters[letter]) for way in order)


def exchange(value, sizes, bits):
    count = sizes[GX] * sizes[GY]
    pairs = [(i, i ^ (1 << bits[i & 1])) for i in range(count)]
    return lax.ppermute(value, BOTH, pairs)


def by_core(first, second):
    zero = lax.axis_index(BOTH) % 2 == 0
    return jnp.where(zero, first, second), jnp.where(zero, second, first)


def gather(halves, sizes, ways):
    mine, other = by_core(*halves)
    arrived = exchange(other, sizes, (0, 0))
    current = jnp.stack(by_core(mine, arrived))[None]
    for bits in zip(*ways):
        current = jnp.concatenate([current, exchange(current, sizes, bits)], 0)
    return current, exchange(current, sizes, (0, 0))


def scatter_sum(mine, other, sizes, ways):
    current = mine.astype(jnp.float32) + exchange(other, sizes, (0, 0)).astype(jnp.float32)
    for bits in reversed(list(zip(*ways))):
        count = current.shape[0] // 2
        arrived = exchange(current[count:].astype(jnp.bfloat16), sizes, bits)
        current = current[:count] + arrived.astype(jnp.float32)
    kept, sent = by_core(current[0, 0], current[0, 1])
    return by_core(kept, exchange(sent.astype(jnp.bfloat16), sizes, (0, 0)).astype(jnp.float32))


def slot(chip, own, way):
    apart = chip ^ own
    total = 0
    for stage, bit in enumerate(way):
        total = total + (((apart >> (bit - 1)) & 1) << stage)
    return total


def chip_slots(count, way):
    return slot(jnp.arange(count), lax.axis_index(BOTH) // 2, way)


class Piece:
    def __init__(self, shapes, rows, step, offsets, columns):
        self.shapes, self.rows, self.step, self.offsets, self.columns = (
            shapes,
            rows,
            step,
            offsets,
            columns,
        )


def assemble(own, arrived, piece, ways):
    chips, _, rows, width = own.shape
    if rows % 8:
        first, second = by_core(own, arrived)
        outs = [jnp.zeros((chips, 2, piece.step, s[1]), jnp.bfloat16) for s in piece.shapes]
        for half, array in enumerate((first, second)):
            array = jnp.take(array, chip_slots(chips, ways[half]), axis=0)
            top = piece.offsets[half]
            for out, source, target, size in piece.columns[half]:
                outs[out] = (
                    outs[out]
                    .at[:, :, top : top + rows, target : target + size]
                    .set(array[:, :, :, source : source + size])
                )
        return [out.reshape(shape) for out, shape in zip(outs, piece.shapes)]
    joined = piece.step == rows
    height = 2 * rows if joined else rows

    def kernel(place, own_ref, arrived_ref, *rest):
        outs, sems = rest[: len(piece.shapes)], rest[len(piece.shapes)]
        core, chip = place[0], place[1]

        def copies(sources):
            def one(q, carry):
                for half in range(2):
                    at = slot(q, chip, ways[half])
                    for j in range(1 if joined else 2):
                        block = sources[half].at[at if joined else 2 * at + j]
                        top = (2 * q + j) * piece.step + piece.offsets[half]
                        top = pl.multiple_of(top, 8)
                        for out, source, target, size in piece.columns[half]:
                            pltpu.make_async_copy(
                                block.at[:, pl.ds(source, size)],
                                outs[out].at[pl.ds(top, height), pl.ds(target, size)],
                                sems.at[out],
                            ).start()
                return carry

            lax.fori_loop(0, chips, one, 0)

        @pl.when(core == 0)
        def _():
            copies((own_ref, arrived_ref))

        @pl.when(core == 1)
        def _():
            copies((arrived_ref, own_ref))

        for out, ref in enumerate(outs):
            pltpu.make_async_copy(ref, ref, sems.at[out]).wait()

    flat = (chips, height, width) if joined else (2 * chips, height, width)
    device = lax.axis_index(BOTH)
    place = jnp.stack([device % 2, device // 2]).astype(jnp.int32)
    total = sum(s[0] * s[1] for s in piece.shapes)
    return pl.pallas_call(
        kernel,
        out_shape=[jax.ShapeDtypeStruct(s, jnp.bfloat16) for s in piece.shapes],
        in_specs=[
            pl.BlockSpec(memory_space=pltpu.SMEM),
            pl.BlockSpec(memory_space=pl.ANY),
            pl.BlockSpec(memory_space=pl.ANY),
        ],
        out_specs=[pl.BlockSpec(memory_space=pltpu.VMEM) for _ in piece.shapes],
        scratch_shapes=[pltpu.SemaphoreType.DMA((len(piece.shapes),))],
        compiler_params=pltpu.CompilerParams(vmem_limit_bytes=24 << 20),
        cost_estimate=pl.CostEstimate(flops=0, bytes_accessed=4 * total, transcendentals=0),
        name="assemble",
    )(place, own.reshape(flat), arrived.reshape(flat))


def spread(products, extra, piece, ways, chips, width):
    rows = piece.rows
    count = len(piece.shapes)

    def product(left, right):
        return lax.dot_general(
            left, right, (((0,), (0,)), ((), ())), preferred_element_type=jnp.float32
        )

    if rows % 8:
        full = [
            (product(*products[i]) if i in products else extra).astype(jnp.bfloat16)
            for i in range(count)
        ]
        halves = []
        for half in range(2):
            array = jnp.zeros((chips, 2, rows, width), jnp.bfloat16)
            top = piece.offsets[half]
            for out, source, target, size in piece.columns[half]:
                part = full[out].reshape(chips, 2, piece.step, -1)
                array = array.at[:, :, :, source : source + size].set(
                    part[:, :, top : top + rows, target : target + size]
                )
            index = jnp.zeros((chips,), jnp.int32).at[chip_slots(chips, ways[half])].set(
                jnp.arange(chips, dtype=jnp.int32)
            )
            halves.append(jnp.take(array, index, axis=0))
        return by_core(*halves)
    joined = piece.step == rows
    height = 2 * rows if joined else rows
    lefts, rights, uses = [], [], {}
    for i, (left, right) in products.items():
        for group, value in ((lefts, left), (rights, right)):
            if not any(value is v for v in group):
                group.append(value)
        uses[i] = (
            [left is v for v in lefts].index(True),
            [right is v for v in rights].index(True),
        )
    operands = lefts + rights + ([extra] if extra is not None else [])

    def kernel(place, *refs):
        left_refs, right_refs = refs[: len(lefts)], refs[len(lefts) : len(lefts) + len(rights)]
        rest = refs[len(lefts) + len(rights) :]
        if extra is not None:
            extra_ref, rest = rest[0], rest[1:]
        mine, other = rest[0], rest[1]
        held = dict(zip(uses, rest[2:]))
        sems = rest[2 + len(uses)]
        core, chip = place[0], place[1]

        def copies(out):
            source_ref = held[out] if out in held else extra_ref

            def send(targets):
                def one(q, carry):
                    for half in range(2):
                        at = slot(q, chip, ways[half])
                        for j in range(1 if joined else 2):
                            block = targets[half].at[at if joined else 2 * at + j]
                            top = (2 * q + j) * piece.step + piece.offsets[half]
                            top = pl.multiple_of(top, 8)
                            for index, source, target, size in piece.columns[half]:
                                if index == out:
                                    pltpu.make_async_copy(
                                        source_ref.at[pl.ds(top, height), pl.ds(target, size)],
                                        block.at[:, pl.ds(source, size)],
                                        sems.at[out],
                                    ).start()
                    return carry

                lax.fori_loop(0, chips, one, 0)

            @pl.when(core == 0)
            def _():
                send((mine, other))

            @pl.when(core == 1)
            def _():
                send((other, mine))

        if extra is not None:
            copies(count - 1)
        for out, (l, r) in uses.items():
            deep, wide = piece.shapes[out]
            tile = 256
            left_ref, right_ref, target_ref = left_refs[l], right_refs[r], held[out]

            def step(i, carry, left_ref=left_ref, right_ref=right_ref, target_ref=target_ref):
                at = pl.multiple_of(i * tile, tile)
                target_ref[pl.ds(at, tile), :] = product(
                    left_ref[:, pl.ds(at, tile)], right_ref[...]
                ).astype(jnp.bfloat16)
                return carry

            lax.fori_loop(0, deep // tile, step, 0)
            copies(out)
        for out in range(count):
            ref = held[out] if out in held else extra_ref
            times = sum(1 for half in range(2) for c in piece.columns[half] if c[0] == out)
            full_columns = sum(c[3] for half in range(2) for c in piece.columns[half] if c[0] == out)
            repeat = full_columns // piece.shapes[out][1] if joined else 1
            for _ in range(max(repeat, 1)):
                pltpu.make_async_copy(ref, ref, sems.at[out]).wait()

    flat = (chips, height, width) if joined else (2 * chips, height, width)
    device = lax.axis_index(BOTH)
    place = jnp.stack([device % 2, device // 2]).astype(jnp.int32)
    total = sum(s[0] * s[1] for s in piece.shapes)
    mine, other = pl.pallas_call(
        kernel,
        out_shape=[jax.ShapeDtypeStruct(flat, jnp.bfloat16)] * 2,
        in_specs=[pl.BlockSpec(memory_space=pltpu.SMEM)]
        + [pl.BlockSpec(memory_space=pltpu.VMEM) for _ in operands],
        out_specs=[pl.BlockSpec(memory_space=pl.ANY)] * 2,
        scratch_shapes=[pltpu.VMEM(piece.shapes[i], jnp.bfloat16) for i in uses]
        + [pltpu.SemaphoreType.DMA((count,))],
        compiler_params=pltpu.CompilerParams(vmem_limit_bytes=40 << 20),
        cost_estimate=pl.CostEstimate(
            flops=512 * total, bytes_accessed=2 * total, transcendentals=0
        ),
        name="spread",
    )(place, *operands)
    shape = (chips, 2, rows, width)
    return mine.reshape(shape), other.reshape(shape)


def body(
    sizes,
    tokens,
    cotangent,
    chosen,
    segment,
    router,
    gain_one,
    gain_two,
    query_weight,
    key_weight,
    value_weight,
    output_weight,
    expand_weight,
    shrink_weight,
):
    row_count, seq_len, width = tokens.shape
    keep_count = chosen.shape[1]
    hidden_units = expand_weight.shape[1]
    chips = sizes[GX] * sizes[GY] // 2
    attn_ways = stage_masks(sizes, ATTN_ORDER)
    expand_ways = stage_masks(sizes, EXPAND_ORDER)
    shrink_ways = stage_masks(sizes, SHRINK_ORDER)
    rows = query_weight.shape[0]
    half_units = hidden_units // 2
    attn_width = 2 * width + LANES
    attn_piece = Piece(
        [(width, width)] * 4 + [(width, LANES)],
        rows,
        rows,
        (0, 0),
        (
            ((0, 0, 0, width), (1, width, 0, width), (4, 2 * width, 0, LANES)),
            ((2, 0, 0, width), (3, width, 0, width)),
        ),
    )
    expand_piece = Piece(
        [(width, hidden_units)],
        rows,
        rows,
        (0, 0),
        (((0, 0, 0, half_units),), ((0, 0, half_units, half_units),)),
    )
    half_rows = shrink_weight.shape[0] // 2
    shrink_piece = Piece(
        [(hidden_units, width)],
        half_rows,
        2 * half_rows,
        (0, half_rows),
        (((0, 0, 0, width),), ((0, 0, 0, width),)),
    )
    small = jnp.stack([router, gain_one, gain_two], axis=1)
    small = jnp.pad(small, ((0, 0), (0, LANES - small.shape[1])))
    attn_halves = (
        jnp.concatenate([query_weight, key_weight, small], axis=1),
        jnp.concatenate([value_weight, output_weight, small], axis=1),
    )
    attn_pair = gather(attn_halves, sizes, attn_ways)
    expand_pair = gather(
        (expand_weight[:, :half_units], expand_weight[:, half_units:]), sizes, expand_ways
    )
    shrink_pair = gather((shrink_weight[:half_rows], shrink_weight[half_rows:]), sizes, shrink_ways)
    query_all, key_all, value_all, output_all, small_all = assemble(
        *attn_pair, attn_piece, attn_ways
    )
    (expand_all,) = assemble(*expand_pair, expand_piece, expand_ways)
    (shrink_all,) = assemble(*shrink_pair, shrink_piece, shrink_ways)
    router_all, gain_one_all, gain_two_all = [small_all[:, i] for i in range(3)]
    head_size = HEAD_DIM
    head_count = width // head_size
    token_count = row_count * keep_count
    picked = chosen[:, :, None] == jnp.arange(seq_len, dtype=chosen.dtype)
    one_hot = picked.astype(jnp.bfloat16)
    hit = jnp.any(picked, axis=1)[:, :, None]

    def take_rows(array):
        taken = jnp.einsum("rks,rsd->rkd", one_hot, array, preferred_element_type=jnp.float32)
        return taken.astype(jnp.bfloat16).reshape(token_count, width)

    def put_rows(array, values):
        values = values.astype(jnp.bfloat16).reshape(row_count, keep_count, width)
        placed = jnp.einsum("rks,rkd->rsd", one_hot, values, preferred_element_type=jnp.float32)
        return jnp.where(hit, placed.astype(jnp.bfloat16), array)

    hidden_low = take_rows(tokens)
    hidden = hidden_low.astype(jnp.float32)
    router_gate = jax.nn.sigmoid(matmul(hidden_low, router_all))
    normed = rms_norm(hidden, gain_one_all.astype(jnp.float32)).astype(jnp.bfloat16)
    head_shape = (row_count, keep_count, head_count, head_size)
    queries = matmul(normed, query_all).astype(jnp.bfloat16).reshape(head_shape)
    key_rows = matmul(normed, key_all).astype(jnp.bfloat16).reshape(head_shape)
    value_rows = matmul(normed, value_all).astype(jnp.bfloat16).reshape(head_shape)
    labels = jnp.sum(jnp.where(picked, segment[:, None, :], 0), axis=-1)
    allowed = (
        (chosen[:, None, :] <= chosen[:, :, None]) & (labels[:, None, :] == labels[:, :, None])
    )[:, None]

    def attn_scores():
        raw_scores = (
            jnp.einsum("rqhd,rkhd->rhqk", queries, key_rows, preferred_element_type=jnp.float32)
            * SCALE
        )
        return jnp.where(allowed, raw_scores, NEGATIVE)

    scores = attn_scores()
    peak = jnp.max(scores, axis=-1, keepdims=True)
    exp_terms = jnp.exp(scores - peak)
    total_mass = jnp.sum(exp_terms, axis=-1, keepdims=True)
    probs_low = (exp_terms / total_mass).astype(jnp.bfloat16)
    log_mass = peak + jnp.log(total_mass)
    attn_mixed = (
        jnp.einsum("rhqk,rkhd->rqhd", probs_low, value_rows, preferred_element_type=jnp.float32)
        .astype(jnp.bfloat16)
        .reshape(token_count, width)
    )
    attn_out = matmul(attn_mixed, output_all)
    middle = hidden + attn_out
    normed_two = rms_norm(middle, gain_two_all.astype(jnp.float32)).astype(jnp.bfloat16)
    pre_act = matmul(normed_two, expand_all)
    gelu_values, gelu_back = jax.vjp(partial(jax.nn.gelu, approximate=True), pre_act)
    activated = gelu_values.astype(jnp.bfloat16)
    mlp_out = matmul(activated, shrink_all)
    branch = attn_out + mlp_out
    updated = hidden + router_gate[:, None] * branch
    out_tokens = put_rows(tokens, updated)
    router_back, gain_one_back, gain_two_back = router_all, gain_one_all, gain_two_all
    query_back, key_back, value_back, output_back = query_all, key_all, value_all, output_all
    expand_back, shrink_back = expand_all, shrink_all
    cot_rows = take_rows(cotangent).astype(jnp.float32)
    grad_branch = router_gate[:, None] * cot_rows
    logit_low = (jnp.sum(cot_rows * branch, axis=-1) * router_gate * (1.0 - router_gate)).astype(
        jnp.bfloat16
    )
    grad_router = matmul(logit_low, hidden_low)
    mlp_low = grad_branch.astype(jnp.bfloat16)
    shrink_parts = scatter_sum(
        *spread({0: (activated, mlp_low)}, None, shrink_piece, shrink_ways, chips, width),
        sizes,
        shrink_ways,
    )
    (grad_pre,) = gelu_back(matmul_right_t(mlp_low, shrink_back))
    pre_low = grad_pre.astype(jnp.bfloat16)
    expand_parts = scatter_sum(
        *spread({0: (normed_two, pre_low)}, None, expand_piece, expand_ways, chips, half_units),
        sizes,
        expand_ways,
    )
    grad_normed_two = matmul_right_t(pre_low, expand_back)
    norm_two_value, norm_two_back = jax.vjp(rms_norm, middle, gain_two_back.astype(jnp.float32))
    grad_middle, grad_gain_two = norm_two_back(grad_normed_two)
    attn_low = (grad_middle + grad_branch).astype(jnp.bfloat16)
    mixed_low = matmul_right_t(attn_low, output_back).astype(jnp.bfloat16).reshape(head_shape)
    probs_again = jnp.exp(attn_scores() - log_mass)
    probs_again_low = probs_again.astype(jnp.bfloat16)
    dvalue_low = (
        jnp.einsum(
            "rhqk,rqhd->rkhd", probs_again_low, mixed_low, preferred_element_type=jnp.float32
        )
        .astype(jnp.bfloat16)
        .reshape(token_count, width)
    )
    grad_probs = jnp.einsum(
        "rqhd,rkhd->rhqk", mixed_low, value_rows, preferred_element_type=jnp.float32
    )
    scores_low = (
        probs_again * (grad_probs - jnp.sum(probs_again * grad_probs, axis=-1, keepdims=True))
    ).astype(jnp.bfloat16)
    dquery_low = (
        (
            jnp.einsum("rhqk,rkhd->rqhd", scores_low, key_rows, preferred_element_type=jnp.float32)
            * SCALE
        )
        .astype(jnp.bfloat16)
        .reshape(token_count, width)
    )
    dkey_low = (
        (
            jnp.einsum("rhqk,rqhd->rkhd", scores_low, queries, preferred_element_type=jnp.float32)
            * SCALE
        )
        .astype(jnp.bfloat16)
        .reshape(token_count, width)
    )
    grad_normed = (
        matmul_right_t(dquery_low, query_back)
        + matmul_right_t(dkey_low, key_back)
        + matmul_right_t(dvalue_low, value_back)
    )
    norm_one_value, norm_one_back = jax.vjp(rms_norm, hidden, gain_one_back.astype(jnp.float32))
    norm_back, grad_gain_one = norm_one_back(grad_normed)
    grad_hidden = (
        cot_rows
        + grad_middle
        + norm_back
        + logit_low.astype(jnp.float32)[:, None] * router_back.astype(jnp.float32)[None, :]
    )
    grad_tokens = put_rows(cotangent, grad_hidden)
    grad_small = jnp.stack([grad_router, grad_gain_one, grad_gain_two], axis=1)
    grad_small = jnp.pad(grad_small, ((0, 0), (0, LANES - grad_small.shape[1])))
    attn_parts = scatter_sum(
        *spread(
            {
                0: (normed, dquery_low),
                1: (normed, dkey_low),
                2: (normed, dvalue_low),
                3: (attn_mixed, attn_low),
            },
            grad_small.astype(jnp.bfloat16),
            attn_piece,
            attn_ways,
            chips,
            attn_width,
        ),
        sizes,
        attn_ways,
    )
    shares = (
        attn_parts[0][:, 2 * width],
        attn_parts[0][:, 2 * width + 1],
        attn_parts[0][:, 2 * width + 2],
        attn_parts[0][:, :width],
        attn_parts[0][:, width : 2 * width],
        attn_parts[1][:, :width],
        attn_parts[1][:, width : 2 * width],
        jnp.concatenate(expand_parts, axis=1),
        jnp.concatenate(shrink_parts, axis=0),
    )
    return (
        out_tokens,
        grad_tokens,
        shares[0],
        shares[1],
        shares[2],
        shares[3],
        shares[4],
        shares[5],
        shares[6],
        shares[7],
        shares[8],
    )


def solution(mesh):
    in_specs = (
        P(("gx", "gy"), None, None),
        P(("gx", "gy"), None, None),
        P(("gx", "gy"), None),
        P(("gx", "gy"), None),
        P(("gx", "gy")),
        P(("gx", "gy")),
        P(("gx", "gy")),
        P(("gx", "gy"), None),
        P(("gx", "gy"), None),
        P(("gx", "gy"), None),
        P(("gx", "gy"), None),
        P(("gx", "gy"), None),
        P(("gx", "gy"), None),
    )
    out_specs = (
        P(("gx", "gy"), None, None),
        P(("gx", "gy"), None, None),
        P(("gx", "gy")),
        P(("gx", "gy")),
        P(("gx", "gy")),
        P(("gx", "gy"), None),
        P(("gx", "gy"), None),
        P(("gx", "gy"), None),
        P(("gx", "gy"), None),
        P(("gx", "gy"), None),
        P(("gx", "gy"), None),
    )
    return jax.shard_map(partial(body, dict(mesh.shape)), mesh=mesh, in_specs=in_specs, out_specs=out_specs, check_vma=False)
```
